32 devices in a mesh: dp: 16 (over z, y, core), mp: 2 (over x).
Axes of the slice: x: 2, y: 2, z: 4, core: 2. Of those that a mesh axis runs over, the one named last changes fastest.
Arguments:
- tokens: bfloat16 [4096, 2048], P(('dp', 'mp')), may hold values from -6 to 6
- doc_lengths: int32 [16, 6], P('dp'), may hold values from 1 to 128, 256 in all within a row
- cotangent: bfloat16 [4096, 2048], P(('dp', 'mp')), may hold values from -6 to 6
- gain_attn: float32 [2048], replicated, may hold values from 0.1 to 1.9
- gain_mlp: float32 [2048], replicated, may hold values from 0.1 to 1.9
- w_qkv: float32 [2048, 3, 2048], P('dp', None, 'mp'), may hold values from -0.1875 to 0.1875
- w_out: float32 [2048, 2048], P('mp', 'dp'), may hold values from -0.375 to 0.375
- w_gate_up: float32 [2048, 2, 5632], P('dp', None, 'mp'), may hold values from -0.125 to 0.125
- w_down: float32 [5632, 2048], P('mp', 'dp'), may hold values from -0.078125 to 0.078125
Outputs:
- block_out: bfloat16 [4096, 2048], P(('dp', 'mp'))
- input_grad: float32 [4096, 2048], P(('dp', 'mp'))
- grad_w_qkv: float32 [2048, 3, 2048], P('dp', None, 'mp')
- grad_w_out: float32 [2048, 2048], P('mp', 'dp')
- grad_w_gate_up: float32 [2048, 2, 5632], P('dp', None, 'mp')
- grad_w_down: float32 [5632, 2048], P('mp', 'dp')
- grad_gain_attn: float32 [2048], replicated
- grad_gain_mlp: float32 [2048], replicated
The draws below stay inside these ranges and needn't reach their ends.
Inputs may be any that keep to these rules, and one draw needn't show every extreme that they name: `doc_lengths`: each packed row's 6 lengths sum to 256, and the longest of each row is exactly 128.
All inputs are finite; a program needn't handle non-finite values.
Results may differ from the reference program's by a relative error of at most 0.014.
The reference program's roundings to bfloat16 on the way count: a program that leaves them out, or rounds other values in their place, can miss the bound.
Values may be sent and summed in bfloat16 or wider, within the bound.
No kernel may reach another device: no remote copies, remote signals or barrier semaphores. Data moves between devices by JAX's collectives and lax.ppermute only.
A program may use at most 256 MiB of HBM per device.

```python
import math
import jax
import jax.numpy as jnp
import numpy as np
from jax import lax

D = 2048
HEADS = 16
HD = 128
FF = 5632
DOCS = 6
ROW = 256
MOST_DOC = 128
TOKENS = 4096
N_DP = 16


def raised(drawn, rng, source, target, blocks, factor):
    def block_of(axis_at):
        return (jnp.arange(drawn.shape[axis_at]) // (drawn.shape[axis_at] // blocks)).reshape((-1,) + (1,) * (drawn.ndim - 1 - axis_at))

    near = jax.random.permutation(rng, blocks)[block_of(target)]
    other_side = (block_of(target) + blocks // 2) % blocks
    return jnp.where((block_of(source) == near) | (block_of(source) == other_side), factor * drawn, drawn)


def block_scale(own_key, dims, shards, least, high):
    gain, own = 1.0, jax.random.fold_in(own_key, 6)
    for dim, shards_of in shards:
        draws = jnp.exp(jax.random.uniform(jax.random.fold_in(own, dim), (shards_of,), jnp.float32, least / len(shards), high / len(shards)))
        gain = gain * jnp.repeat(draws, dims[dim] // shards_of).reshape([-1 if axis == dim else 1 for axis in range(len(dims))])
    return gain


def profile(amount, total, bound, slope):
    portions = [(1 << 20) // math.isqrt(standing ** slope) + 1 for standing in range(2, amount + 1)]
    surplus, counts = total - bound - (amount - 1), [1] * (amount - 1)
    while surplus > 0:
        candidates = [i for i in range(amount - 1) if counts[i] < bound]
        whole, remaining = sum([portions[i] for i in candidates]), surplus
        for i in candidates:
            addition = min(bound - counts[i], max(1, remaining * portions[i] // whole), surplus)
            counts[i] = counts[i] + addition
            surplus = surplus - addition
    return np.array([bound] + counts)


def ragged_sizes(stream_key, count, total, bound, lean):
    if count == 2:
        one = jax.random.randint(stream_key, (), max(1, total - bound), min(bound, total - 1) + 1)
        return jnp.stack([one, total - one])
    sizes = jnp.asarray(profile(count, total, bound, lean), jnp.int32)
    twos = (count - 1) // 2
    giver, sink = sizes[1:1 + 2 * twos:2], sizes[2:2 + 2 * twos:2]
    room = jnp.minimum(giver - 1, bound - sink)
    passed = jax.random.randint(jax.random.fold_in(stream_key, 1), (twos,), 0, 1 << 20) % (room + 1)
    sizes = sizes.at[1:1 + 2 * twos:2].set(giver - passed).at[2:2 + 2 * twos:2].set(sink + passed)
    return sizes[jax.random.permutation(jax.random.fold_in(stream_key, 2), count)]


def gaussian(stream_key, extent, spread, bound, split=(), held_as=jnp.bfloat16):
    loudness = block_scale(stream_key, extent, split, -0.22, 0.18) if split else 1.0
    entries = jax.random.normal(stream_key, extent, jnp.float32) * spread * loudness
    return jnp.minimum(jnp.maximum(entries, -bound), bound).astype(held_as)


def bell_draw_with(rng, extent, width, bound, cuts, heavy, kind=jnp.bfloat16):
    values = width * jax.random.normal(rng, extent, jnp.float32)
    if cuts:
        values = values * block_scale(rng, extent, cuts, -0.22, 0.18)
    return jnp.clip(raised(values, jax.random.fold_in(rng, 3), *heavy), -bound, bound).astype(kind)


def setup_inputs(seed: int = 0) -> dict:
    splits = jax.random.split(jax.random.key(seed), 10)
    tokens = bell_draw_with(splits[0], (TOKENS, D), 1.0, 6.0, ((0, 32),), (0, 1, 32, 2.75))
    doc_lengths = jax.vmap(lambda own: ragged_sizes(own, DOCS, ROW, MOST_DOC, 2))(jax.random.split(splits[1], N_DP)).reshape((N_DP, DOCS)).astype(jnp.int32)
    cotangent = bell_draw_with(splits[2], (TOKENS, D), 1.0, 6.0, ((0, 32),), (0, 1, 32, 2.75))
    gain_attn = jnp.clip(1.0 + 0.18 * jax.random.normal(splits[3], (D,), jnp.float32), 0.1, 1.9)
    gain_mlp = jnp.clip(1.0 + 0.18 * jax.random.normal(splits[4], (D,), jnp.float32), 0.1, 1.9)
    w_qkv = gaussian(splits[5], (D, 3, D), (D // 2) ** -0.5, 0.1875, ((0, 16), (2, 2)), jnp.float32)
    w_out = gaussian(splits[6], (D, D), (D // 8) ** -0.5, 0.375, ((0, 2), (1, 16)), jnp.float32)
    w_gate_up = gaussian(splits[7], (D, 2, FF), D ** -0.5, 0.125, ((0, 16), (2, 2)), jnp.float32)
    w_down = gaussian(splits[8], (FF, D), FF ** -0.5, 0.078125, ((0, 2), (1, 16)), jnp.float32)
    return dict(tokens=tokens, doc_lengths=doc_lengths, cotangent=cotangent, gain_attn=gain_attn, gain_mlp=gain_mlp, w_qkv=w_qkv, w_out=w_out, w_gate_up=w_gate_up, w_down=w_down)


@jax.custom_vjp
def low(v):
    return lax.optimization_barrier(v.astype(jnp.bfloat16)).astype(jnp.float32)

@jax.custom_vjp
def low_back(v):
    return v

def low_keep(v):
    return (low(v), None)

def low_pass(kept, grad):
    return (grad,)

def back_keep(v):
    return (v, None)

def back_low(kept, grad):
    return (low(grad),)
low.defvjp(low_keep, low_pass)
low_back.defvjp(back_keep, back_low)
EPSILON = 1e-05
MASKED = -1e+30
HIGHEST = lax.Precision.HIGHEST

def row_layout(lengths):
    doc_ends = jnp.cumsum(lengths).astype(jnp.int32)
    places = jnp.arange(ROW, dtype=jnp.int32)
    segment = lax.optimization_barrier(jnp.sum((places[:, None] >= doc_ends[None, :]).astype(jnp.int32), axis=1)).astype(jnp.int32)
    starts = (doc_ends - lengths).astype(jnp.int32)
    chosen = segment[:, None] == jnp.arange(lengths.shape[0], dtype=jnp.int32)[None, :]
    doc_start = lax.optimization_barrier(jnp.sum(jnp.where(chosen, starts[None, :], 0), axis=1)).astype(jnp.int32)
    return (segment, places - doc_start)

def rotary_tables(offsets, head_size):
    half_size = head_size // 2
    frequency = 10000.0 ** (-2.0 * jnp.arange(half_size, dtype=jnp.float32) / head_size)
    angles = offsets.astype(jnp.float32)[:, None] * frequency[None, :]
    return (jnp.cos(angles), jnp.sin(angles))

def rotate(field, cosine, sine_table):
    half_size = field.shape[-1] // 2
    front_half = field[..., :half_size]
    back_half = field[..., half_size:]
    cos_rows = cosine[:, None, :]
    sin_rows = sine_table[:, None, :]
    return jnp.concatenate([front_half * cos_rows - back_half * sin_rows, back_half * cos_rows + front_half * sin_rows], axis=-1)

def rms_norm(field, gain_vec):
    return field * lax.rsqrt(lax.optimization_barrier(jnp.mean(field * field, axis=-1, keepdims=True)) + EPSILON) * gain_vec

def attend(projected, segment, offsets):
    cosine, sine_table = rotary_tables(offsets, HD)
    queries = low(rotate(projected[0], cosine, sine_table))
    keys_rot = low(rotate(projected[1], cosine, sine_table))
    values_low = low(projected[2])
    raw_scores = low_back(jnp.einsum('qhe,khe->hqk', queries, keys_rot, precision=HIGHEST))
    places = jnp.arange(ROW, dtype=jnp.int32)
    allowed = (segment[:, None] == segment[None, :]) & (places[None, :] <= places[:, None])
    scores = jnp.where(allowed[None], raw_scores * HD ** (-0.5), MASKED)
    attn_probs = jax.nn.softmax(scores, axis=-1)
    mixed = jnp.einsum('hqk,khe->qhe', low(attn_probs), values_low, precision=HIGHEST)
    return low_back(low(mixed)).reshape(ROW, HEADS * HD)

def forward_row(resid_in, segment, offsets, gain_attn, gain_mlp, weights):
    w_qkv, w_out, w_gate_up, w_down = weights
    normed_attn = low(rms_norm(resid_in, gain_attn))
    projected = low_back(jnp.einsum('td,dce->cte', normed_attn, w_qkv, precision=HIGHEST))
    mixed = attend(projected.reshape(3, ROW, HEADS, HD), segment, offsets)
    resid_mid = resid_in + low_back(jnp.dot(mixed, w_out, precision=HIGHEST))
    normed_mlp = low(rms_norm(resid_mid, gain_mlp))
    gate_up = low_back(jnp.einsum('td,dcf->ctf', normed_mlp, w_gate_up, precision=HIGHEST))
    hidden = low(jax.nn.silu(gate_up[0]) * gate_up[1])
    return resid_mid + low_back(jnp.dot(hidden, w_down, precision=HIGHEST))

def reference(tokens, doc_lengths, cotangent, gain_attn, gain_mlp, w_qkv, w_out, w_gate_up, w_down):
    segment, offsets = jax.vmap(row_layout)(doc_lengths)
    rows_in = tokens.astype(jnp.float32).reshape(-1, ROW, D)

    def whole_block(resid_rows, gain_a, gain_m, weight_qkv, weight_out, weight_gu, weight_down):
        weights = (low(weight_qkv), low(weight_out), low(weight_gu), low(weight_down))

        def one_row(pieces):
            return forward_row(pieces[0], pieces[1], pieces[2], gain_a, gain_m, weights)
        return lax.map(jax.checkpoint(one_row), (resid_rows, segment, offsets))
    result, pullback = jax.vjp(whole_block, rows_in, gain_attn, gain_mlp, w_qkv, w_out, w_gate_up, w_down)
    grads = pullback(cotangent.astype(jnp.float32).reshape(-1, ROW, D))
    return (result.reshape(-1, D).astype(jnp.bfloat16), grads[0].reshape(-1, D), grads[3], grads[4], grads[5], grads[6], grads[1], grads[2])
```

```python
import jax
import jax.numpy as jnp
from jax import lax
from jax.sharding import PartitionSpec as P

HD = 128


EPSILON = 1e-05
MASKED = -1e30


def row_layout(lengths, row_len):
    doc_ends = jnp.cumsum(lengths)
    places = jnp.arange(row_len, dtype=jnp.int32)
    segment = jnp.sum((places[:, None] >= doc_ends[None, :]).astype(jnp.int32), axis=1)
    starts = doc_ends - lengths
    chosen = segment[:, None] == jnp.arange(lengths.shape[0], dtype=jnp.int32)[None, :]
    doc_start = jnp.sum(jnp.where(chosen, starts[None, :], 0), axis=1)
    return (segment, places - doc_start, places)


def rotary_tables(offsets, head_size):
    half_size = head_size // 2
    frequency = 10000.0 ** (-2.0 * jnp.arange(half_size, dtype=jnp.float32) / head_size)
    angles = offsets.astype(jnp.float32)[:, None] * frequency[None, :]
    return (jnp.cos(angles), jnp.sin(angles))


def rotate(field, cosine, sine_table):
    half_size = field.shape[-1] // 2
    front_half = field[..., :half_size]
    back_half = field[..., half_size:]
    cos_rows = cosine[:, None, :]
    sin_rows = sine_table[:, None, :]
    return jnp.concatenate(
        [
            front_half * cos_rows - back_half * sin_rows,
            back_half * cos_rows + front_half * sin_rows,
        ],
        axis=-1,
    )


def rotate_back(gradient, cosine, sine_table):
    half_size = gradient.shape[-1] // 2
    front_half = gradient[..., :half_size]
    back_half = gradient[..., half_size:]
    cos_rows = cosine[:, None, :]
    sin_rows = sine_table[:, None, :]
    return jnp.concatenate(
        [
            front_half * cos_rows + back_half * sin_rows,
            back_half * cos_rows - front_half * sin_rows,
        ],
        axis=-1,
    )


def norm_scale(field):
    return lax.rsqrt(jnp.mean(field * field, axis=-1, keepdims=True) + EPSILON)


def norm_back(grad_normed, field, gain_vec):
    inverse = norm_scale(field)
    normed = field * inverse
    scaled = grad_normed * gain_vec
    grad_field = inverse * (scaled - normed * jnp.mean(scaled * normed, axis=-1, keepdims=True))
    return (grad_field, jnp.sum(grad_normed * normed, axis=0))


def masked_scores(query_block, keys_rot, seg_rows, segment, place_rows, places, scale):
    raw_scores = jnp.einsum(
        "qhe,khe->hqk", query_block, keys_rot, preferred_element_type=jnp.float32
    )
    allowed = (seg_rows[:, None] == segment[None, :]) & (places[None, :] <= place_rows[:, None])
    return jnp.where(allowed[None], raw_scores * scale, MASKED)


def scatter_sum(gradient, dimension):
    total = lax.psum_scatter(
        gradient.astype(jnp.bfloat16), "dp", scatter_dimension=dimension, tiled=True
    )
    return total.astype(jnp.float32)


def on_device(tokens, doc_lengths, cotangent, gain_attn, gain_mlp, w_qkv, w_out, w_gate_up, w_down):
    local_rows = tokens.shape[0]
    row_len = local_rows * lax.axis_size("mp")
    segment, offsets, places = row_layout(doc_lengths[0], row_len)
    cosine, sine_table = rotary_tables(offsets, HD)
    scale = HD ** (-0.5)
    block_count = max(1, row_len // 512)
    block_len = row_len // block_count
    block_starts = jnp.arange(block_count, dtype=jnp.int32) * block_len
    masters = (
        w_qkv.astype(jnp.bfloat16),
        w_out.astype(jnp.bfloat16),
        w_gate_up.astype(jnp.bfloat16),
        w_down.astype(jnp.bfloat16),
    )
    w_qkv_all, w_out_all, w_gu_all, w_down_all = (
        lax.all_gather(masters[0], "dp", axis=0, tiled=True),
        lax.all_gather(masters[1], "dp", axis=1, tiled=True),
        lax.all_gather(masters[2], "dp", axis=0, tiled=True),
        lax.all_gather(masters[3], "dp", axis=1, tiled=True),
    )
    resid_in = tokens.astype(jnp.float32)
    normed_attn = (resid_in * norm_scale(resid_in) * gain_attn).astype(jnp.bfloat16)
    attn_rows = lax.all_gather(normed_attn, "mp", axis=0, tiled=True)
    projected = jnp.einsum("td,dce->cte", attn_rows, w_qkv_all, preferred_element_type=jnp.float32)
    local_dim = projected.shape[2]
    local_heads = local_dim // HD
    projected = projected.reshape(3, row_len, local_heads, HD)
    queries = rotate(projected[0], cosine, sine_table).astype(jnp.bfloat16)
    keys_rot = rotate(projected[1], cosine, sine_table).astype(jnp.bfloat16)
    values_low = projected[2].astype(jnp.bfloat16)

    def forward_block(row_start):
        scores = masked_scores(queries, keys_rot, segment, segment, places, places, scale)
        row_max = jnp.max(scores, axis=-1, keepdims=True)
        exp_scores = jnp.exp(scores - row_max)
        denominator = jnp.sum(exp_scores, axis=-1, keepdims=True)
        attn_probs = (exp_scores / denominator).astype(jnp.bfloat16)
        mixed = jnp.einsum(
            "hqk,khe->qhe", attn_probs, values_low, preferred_element_type=jnp.float32
        )
        return (mixed.astype(jnp.bfloat16), (row_max + jnp.log(denominator))[..., 0])

    mixed_blocks, log_total = lax.map(forward_block, block_starts)
    mixed_rows = mixed_blocks.reshape(row_len, local_dim)
    part_rows = mixed_rows
    attn_part = lax.psum_scatter(
        jnp.dot(part_rows, w_out_all, preferred_element_type=jnp.float32),
        "mp",
        scatter_dimension=0,
        tiled=True,
    )
    resid_mid = resid_in + attn_part
    normed_mlp = (resid_mid * norm_scale(resid_mid) * gain_mlp).astype(jnp.bfloat16)
    mlp_rows = lax.all_gather(normed_mlp, "mp", axis=0, tiled=True)
    gate_up = jnp.einsum("td,dcf->ctf", mlp_rows, w_gu_all, preferred_element_type=jnp.float32)
    gate_sig = jax.nn.sigmoid(gate_up[0])
    gate_act = gate_up[0] * gate_sig
    hidden = (gate_act * gate_up[1]).astype(jnp.bfloat16)
    part_rows = hidden
    mlp_part = lax.psum_scatter(
        jnp.dot(part_rows, w_down_all, preferred_element_type=jnp.float32).astype(jnp.bfloat16),
        "mp",
        scatter_dimension=0,
        tiled=True,
    ).astype(jnp.float32)
    block_out = (resid_mid + mlp_part).astype(jnp.bfloat16)
    w_qkv_all, w_out_all, w_gu_all, w_down_all = (
        lax.all_gather(masters[0], "dp", axis=0, tiled=True),
        lax.all_gather(masters[1], "dp", axis=1, tiled=True),
        lax.all_gather(masters[2], "dp", axis=0, tiled=True),
        lax.all_gather(masters[3], "dp", axis=1, tiled=True),
    )
    grad_rows = lax.all_gather(cotangent, "mp", axis=0, tiled=True)
    grad_down = jnp.einsum("tf,td->fd", hidden, grad_rows, preferred_element_type=jnp.float32)
    d_hidden = jnp.einsum("td,fd->tf", grad_rows, w_down_all, preferred_element_type=jnp.float32)
    d_gate = d_hidden * gate_up[1] * gate_sig * (1.0 + gate_up[0] * (1.0 - gate_sig))
    d_up = d_hidden * gate_act
    d_gate_up = jnp.stack([d_gate, d_up]).astype(jnp.bfloat16)
    grad_gate_up = jnp.einsum(
        "td,ctf->dcf", mlp_rows, d_gate_up, preferred_element_type=jnp.float32
    )
    mlp_sums = (grad_gate_up, grad_down)
    part_rows = d_gate_up
    d_normed_mlp = lax.psum_scatter(
        jnp.einsum("ctf,dcf->td", part_rows, w_gu_all, preferred_element_type=jnp.float32),
        "mp",
        scatter_dimension=0,
        tiled=True,
    )
    d_resid_norm, gain_mlp_part = norm_back(d_normed_mlp, resid_mid, gain_mlp)
    d_resid_mid = d_resid_norm + cotangent.astype(jnp.float32)
    attn_grad_rows = lax.all_gather(d_resid_mid.astype(jnp.bfloat16), "mp", axis=0, tiled=True)
    grad_out = jnp.einsum(
        "te,td->ed", mixed_rows, attn_grad_rows, preferred_element_type=jnp.float32
    )
    d_mixed = jnp.einsum("td,ed->te", attn_grad_rows, w_out_all, preferred_element_type=jnp.float32)
    d_mixed = d_mixed.astype(jnp.bfloat16).reshape(row_len, local_heads, HD)

    def backward_block(running, pieces):
        d_keys_sum, d_values_sum = running
        row_start, log_block = pieces
        scores = masked_scores(queries, keys_rot, segment, segment, places, places, scale)
        attn_probs = jnp.exp(scores - log_block[..., None])
        d_probs = jnp.einsum(
            "qhe,khe->hqk", d_mixed, values_low, preferred_element_type=jnp.float32
        )
        row_dot = jnp.sum(attn_probs * d_probs, axis=-1, keepdims=True)
        d_raw = (attn_probs * (d_probs - row_dot) * scale).astype(jnp.bfloat16)
        d_query_block = jnp.einsum(
            "hqk,khe->qhe", d_raw, keys_rot, preferred_element_type=jnp.float32
        )
        d_keys_sum = d_keys_sum + jnp.einsum(
            "hqk,qhe->khe", d_raw, queries, preferred_element_type=jnp.float32
        )
        d_values_sum = d_values_sum + jnp.einsum(
            "hqk,qhe->khe",
            attn_probs.astype(jnp.bfloat16),
            d_mixed,
            preferred_element_type=jnp.float32,
        )
        return ((d_keys_sum, d_values_sum), d_query_block)

    zero_heads = jnp.zeros((row_len, local_heads, HD), jnp.float32)
    (d_keys, d_values), d_query_blocks = lax.scan(
        backward_block, (zero_heads, zero_heads), (block_starts, log_total)
    )
    d_queries = d_query_blocks.reshape(row_len, local_heads, HD)
    d_projected = jnp.stack(
        [
            rotate_back(d_queries, cosine, sine_table),
            rotate_back(d_keys, cosine, sine_table),
            d_values,
        ]
    )
    d_projected = d_projected.astype(jnp.bfloat16).reshape(3, row_len, local_dim)
    grad_qkv = jnp.einsum("td,cte->dce", attn_rows, d_projected, preferred_element_type=jnp.float32)
    part_rows = d_projected
    d_normed_attn = lax.psum_scatter(
        jnp.einsum("cte,dce->td", part_rows, w_qkv_all, preferred_element_type=jnp.float32).astype(
            jnp.bfloat16
        ),
        "mp",
        scatter_dimension=0,
        tiled=True,
    ).astype(jnp.float32)
    d_resid_first, gain_attn_part = norm_back(d_normed_attn, resid_in, gain_attn)
    input_grad = d_resid_mid + d_resid_first
    gain_totals = lax.psum((gain_attn_part, gain_mlp_part), ("dp", "mp"))
    weight_sums = (
        scatter_sum(grad_qkv, 0),
        scatter_sum(grad_out, 1),
        scatter_sum(mlp_sums[0], 0),
        scatter_sum(mlp_sums[1], 1),
    )
    return (
        block_out,
        input_grad,
        weight_sums[0],
        weight_sums[1],
        weight_sums[2],
        weight_sums[3],
        gain_totals[0],
        gain_totals[1],
    )


def solution(mesh):
    return jax.shard_map(
        on_device,
        mesh=mesh,
        in_specs=(
            P(("dp", "mp"), None),
            P("dp", None),
            P(("dp", "mp"), None),
            P(),
            P(),
            P("dp", None, "mp"),
            P("mp", "dp"),
            P("dp", None, "mp"),
            P("mp", "dp"),
        ),
        out_specs=(
            P(("dp", "mp"), None),
            P(("dp", "mp"), None),
            P("dp", None, "mp"),
            P("mp", "dp"),
            P("dp", None, "mp"),
            P("mp", "dp"),
            P(),
            P(),
        ),
        check_vma=False,
    )
```

```python
import jax
import jax.numpy as jnp
from jax import lax
from jax.sharding import PartitionSpec as P

HD = 128
EPSILON = 1e-05
MASKED = -1e30
F32 = jnp.float32
BF16 = jnp.bfloat16


class Plan:
    def __init__(self):
        self.n_dp = lax.axis_size("dp")
        self.n_mp = lax.axis_size("mp")
        self.bits = self.n_dp.bit_length() - 1
        self.core = 1
        near = 2 if self.bits == 4 else 1
        self.near = 1 << near
        self.outer = [b for b in reversed(range(self.bits)) if b not in (0, near)]
        self.blocks = 1 << len(self.outer)
        self.dp = lax.axis_index("dp")
        self.mp = lax.axis_index("mp")
        self.quarter = ((self.dp >> near) & 1) * 2 + (self.dp & 1)
        self.order = tuple(reversed(self.outer)) + (near, 0)

    def swap(self, value, dp_mask, mp_mask=0):
        n_mp = self.n_mp
        pairs = [
            (d * n_mp + m, (d ^ dp_mask) * n_mp + (m ^ mp_mask))
            for d in range(self.n_dp)
            for m in range(n_mp)
        ]
        return lax.ppermute(value, ("dp", "mp"), pairs)

    def quad(self, r):
        return (self.near if r & 2 else 0) | (r & 1)

    def my_bit(self, b):
        return ((self.dp >> b) & 1) == 1

    def to_relative(self, value):
        lead = value.shape[:-1]
        n = len(lead)
        v = value.reshape(lead + (2,) * self.bits + (-1,))
        for b in self.outer:
            axis = n + self.bits - 1 - b
            v = jnp.where(self.my_bit(b), jnp.flip(v, axis), v)
        axes = tuple(range(n)) + tuple(n + self.bits - 1 - b for b in self.order)
        return v.transpose(axes + (n + self.bits,)).reshape(value.shape)

    def from_relative(self, value):
        lead = value.shape[:-1]
        n = len(lead)
        v = value.reshape(lead + (2,) * self.bits + (-1,))
        source = [0] * self.bits
        for place, b in enumerate(self.order):
            source[self.bits - 1 - b] = n + place
        v = v.transpose(tuple(range(n)) + tuple(source) + (n + self.bits,))
        for b in self.outer:
            axis = n + self.bits - 1 - b
            v = jnp.where(self.my_bit(b), jnp.flip(v, axis), v)
        return v.reshape(value.shape)

    def quarters_absolute(self, pieces):
        p0, p1, p2, p3 = pieces
        core = (self.quarter & 1) == 1
        near = self.quarter >= 2
        a0, a1 = jnp.where(core, p1, p0), jnp.where(core, p0, p1)
        a2, a3 = jnp.where(core, p3, p2), jnp.where(core, p2, p3)
        return [
            jnp.where(near, a2, a0),
            jnp.where(near, a3, a1),
            jnp.where(near, a0, a2),
            jnp.where(near, a1, a3),
        ]

    def exchange_quarters(self, stacked):
        pieces = []
        for r in range(4):
            part = lax.dynamic_index_in_dim(stacked, self.quarter ^ r, 0, keepdims=False)
            pieces.append(part if r == 0 else self.swap(part, self.quad(r)))
        return self.quarters_absolute(pieces)

    def gather_outer(self, own, axis):
        blocks = [own]
        for b in self.outer:
            blocks = blocks + [self.swap(v, 1 << b) for v in blocks]
        return jnp.concatenate(blocks, axis=axis)

    def scatter_outer(self, make):
        total = {}

        def block(i, received):
            value = make(i)
            for r in received:
                value = value + r.astype(F32)
            return value

        got = {i: [] for i in range(self.blocks)}
        half = self.blocks // 2
        for b in reversed(self.outer):
            for i in reversed(range(half, 2 * half)):
                sent = block(i, got[i]).astype(BF16)
                got[i - half].append(self.swap(sent, 1 << b))
            half //= 2
        return block(0, got[0])

    def gather_rows(self, own):
        part = [
            own,
            self.swap(own, 0, 1),
            self.swap(own, self.near),
            self.swap(own, self.near, 1),
        ]
        other = [self.swap(p, self.core) for p in part]
        return jnp.concatenate(part + other, axis=0)

    def scatter_rows(self, product, rows):
        half = rows // 2
        sent = product(slice(half, rows)).astype(BF16)
        total = product(slice(0, half)) + self.swap(sent, self.core).astype(F32)
        part = half // 4
        pieces = [total[i * part : (i + 1) * part] for i in range(4)]
        far = self.swap(pieces[3].astype(BF16), self.near, 1)
        near = self.swap(pieces[2].astype(BF16), self.near)
        side = self.swap(pieces[1].astype(BF16), 0, 1)
        return pieces[0] + (side.astype(F32) + near.astype(F32) + far.astype(F32))

    def sum_all(self, value):
        for b in range(self.bits):
            value = value + self.swap(value, 1 << b)
        return value + self.swap(value, 0, 1)


def row_layout(lengths, places):
    doc_ends = jnp.cumsum(lengths, axis=-1)
    segment = jnp.sum((places[None, :, None] >= doc_ends[:, None, :]).astype(jnp.int32), axis=-1)
    starts = doc_ends - lengths
    chosen = segment[..., None] == jnp.arange(lengths.shape[-1], dtype=jnp.int32)
    doc_start = jnp.sum(jnp.where(chosen, starts[:, None, :], 0), axis=-1)
    return segment, places[None, :] - doc_start


def rotary_tables(offsets, head_size):
    half_size = head_size // 2
    frequency = 10000.0 ** (-2.0 * jnp.arange(half_size, dtype=F32) / head_size)
    angles = offsets.astype(F32)[..., None] * frequency
    return jnp.cos(angles), jnp.sin(angles)


def rotate(field, cos_rows, sin_rows):
    half_size = field.shape[-1] // 2
    front, back = field[..., :half_size], field[..., half_size:]
    return jnp.concatenate(
        [front * cos_rows - back * sin_rows, back * cos_rows + front * sin_rows], axis=-1
    )


def norm_scale(field):
    return lax.rsqrt(jnp.mean(field * field, axis=-1, keepdims=True) + EPSILON)


def norm_back(grad_normed, field, gain_vec):
    inverse = norm_scale(field)
    normed = field * inverse
    scaled = grad_normed * gain_vec
    grad_field = inverse * (scaled - normed * jnp.mean(scaled * normed, axis=-1, keepdims=True))
    return grad_field, jnp.sum(grad_normed * normed, axis=0)


def dot(a, b, dims):
    return lax.dot_general(a, b, (dims, ((), ())), preferred_element_type=F32)


NN = ((1,), (0,))
NT = ((1,), (1,))
TN = ((0,), (0,))


def on_device(tokens, doc_lengths, cotangent, gain_attn, gain_mlp, w_qkv, w_out, w_gate_up, w_down):
    plan = Plan()
    mine, width = tokens.shape
    own_rows = w_qkv.shape[0]
    rows = mine * 8
    row_len = mine * plan.n_mp
    scale = HD ** (-0.5)
    span = width // plan.blocks

    qkv_parts = w_qkv.astype(BF16).reshape(own_rows, 3, 4, -1).transpose(2, 0, 1, 3)
    qkv_parts = qkv_parts.reshape(4, own_rows, -1)
    gu_parts = w_gate_up.astype(BF16).reshape(own_rows, 2, 4, -1).transpose(2, 0, 1, 3)
    gu_parts = gu_parts.reshape(4, own_rows, -1)
    out_parts = w_out.astype(BF16).reshape(4, -1, own_rows)
    down_parts = w_down.astype(BF16).reshape(4, -1, own_rows)
    units = down_parts.shape[1]

    resid_in = plan.to_relative(tokens.astype(F32))
    grad_low = plan.to_relative(cotangent)
    gain_a = plan.to_relative(gain_attn)
    gain_m = plan.to_relative(gain_mlp)
    normed_attn = (resid_in * norm_scale(resid_in) * gain_a).astype(BF16)
    attn_rows = plan.gather_rows(normed_attn)

    wq = plan.gather_outer(jnp.concatenate(plan.exchange_quarters(qkv_parts), axis=0), 0)
    wo = plan.gather_outer(jnp.concatenate(plan.exchange_quarters(out_parts), axis=1), 1)
    wgu = plan.gather_outer(jnp.concatenate(plan.exchange_quarters(gu_parts), axis=0), 0)
    wd = plan.gather_outer(jnp.concatenate(plan.exchange_quarters(down_parts), axis=1), 1)
    grad_rows = plan.gather_rows(grad_low)

    near_lengths = jnp.concatenate([doc_lengths, plan.swap(doc_lengths, plan.near)], axis=0)
    lengths = jnp.concatenate([near_lengths, plan.swap(near_lengths, plan.core)], axis=0)
    part = jnp.arange(mine, dtype=jnp.int32)
    places = jnp.concatenate([part + plan.mp * mine, part + (1 - plan.mp) * mine])
    segment, offsets = row_layout(lengths, places)
    cosine, sine = rotary_tables(offsets, HD)
    cosine, sine = cosine[:, :, None, :], sine[:, :, None, :]
    allowed = (segment[:, :, None] == segment[:, None, :]) & (
        places[None, None, :] <= places[None, :, None]
    )
    allowed = allowed[:, None]

    projected = dot(attn_rows, wq, NN).reshape(4, row_len, 3, -1, HD)
    heads = projected.shape[3]
    queries = rotate(projected[:, :, 0], cosine, sine).astype(BF16)
    keys_rot = rotate(projected[:, :, 1], cosine, sine).astype(BF16)
    values_low = projected[:, :, 2].astype(BF16)

    def all_scores():
        raw = jnp.einsum("rqhe,rkhe->rhqk", queries, keys_rot, preferred_element_type=F32)
        return jnp.where(allowed, raw * scale, MASKED)

    probs = jax.nn.softmax(all_scores(), axis=-1)
    probs_low = probs.astype(BF16)
    mixed = jnp.einsum("rhqk,rkhe->rqhe", probs_low, values_low, preferred_element_type=F32)
    mixed = mixed.astype(BF16).reshape(rows, heads * HD)

    resid_mid = resid_in + plan.scatter_rows(lambda s: dot(mixed[s], wo, NN), rows)
    normed_mlp = (resid_mid * norm_scale(resid_mid) * gain_m).astype(BF16)
    mlp_rows = plan.gather_rows(normed_mlp)
    gate_up = dot(mlp_rows, wgu, NN)
    gate, up = gate_up[:, :units], gate_up[:, units:]
    gate_sig = jax.nn.sigmoid(gate)
    gate_act = gate * gate_sig
    hidden = (gate_act * up).astype(BF16)
    block_out = resid_mid + plan.scatter_rows(lambda s: dot(hidden[s], wd, NN), rows)
    block_out = plan.from_relative(block_out.astype(BF16))

    def cols(value, i):
        return value[:, i * span : (i + 1) * span]

    sum_down = plan.scatter_outer(lambda i: dot(hidden, cols(grad_rows, i), TN))
    d_hidden = dot(grad_rows, wd, NT)
    d_gate = d_hidden * up * gate_sig * (1.0 + gate * (1.0 - gate_sig))
    d_up = d_hidden * gate_act
    d_gate_up = jnp.concatenate([d_gate, d_up], axis=1).astype(BF16)
    d_normed = plan.scatter_rows(lambda s: dot(d_gate_up[s], wgu, NT), rows)
    sum_gu = plan.scatter_outer(lambda i: dot(cols(mlp_rows, i), d_gate_up, TN))
    d_norm_mid, gain_mlp_part = norm_back(d_normed, resid_mid, gain_m)
    d_resid_mid = d_norm_mid + grad_low.astype(F32)
    attn_grad_rows = plan.gather_rows(d_resid_mid.astype(BF16))
    sum_out = plan.scatter_outer(lambda i: dot(mixed, cols(attn_grad_rows, i), TN))

    d_mixed = dot(attn_grad_rows, wo, NT).astype(BF16).reshape(4, row_len, heads, HD)
    d_probs = jnp.einsum("rqhe,rkhe->rhqk", d_mixed, values_low, preferred_element_type=F32)
    row_dot = jnp.sum(probs * d_probs, axis=-1, keepdims=True)
    d_raw = (probs * (d_probs - row_dot) * scale).astype(BF16)
    d_query = jnp.einsum("rhqk,rkhe->rqhe", d_raw, keys_rot, preferred_element_type=F32)
    d_key = jnp.einsum("rhqk,rqhe->rkhe", d_raw, queries, preferred_element_type=F32)
    d_value = jnp.einsum("rhqk,rqhe->rkhe", probs_low, d_mixed, preferred_element_type=F32)
    d_projected = jnp.stack(
        [rotate(d_query, cosine, -sine), rotate(d_key, cosine, -sine), d_value], axis=2
    )
    d_projected = d_projected.astype(BF16).reshape(rows, -1)
    sum_qkv = plan.scatter_outer(lambda i: dot(cols(attn_rows, i), d_projected, TN))
    d_normed_attn = plan.scatter_rows(lambda s: dot(d_projected[s], wq, NT), rows)
    d_first, gain_attn_part = norm_back(d_normed_attn, resid_in, gain_a)
    input_grad = plan.from_relative(d_resid_mid + d_first)
    gains = plan.from_relative(jnp.stack([gain_attn_part, gain_mlp_part]))
    gains = plan.sum_all(gains)

    def rows_home(total, ways):
        parts = total.astype(BF16).reshape(4, own_rows, -1)
        parts = jnp.stack(plan.exchange_quarters(parts)).reshape(4, own_rows, ways, -1)
        return parts.transpose(1, 2, 0, 3).reshape(own_rows, ways, -1).astype(F32)

    def cols_home(total):
        parts = total.astype(BF16).reshape(-1, 4, own_rows).transpose(1, 0, 2)
        return jnp.concatenate(plan.exchange_quarters(parts), axis=0).astype(F32)

    return (
        block_out,
        input_grad,
        rows_home(sum_qkv, 3),
        cols_home(sum_out),
        rows_home(sum_gu, 2),
        cols_home(sum_down),
        gains[0],
        gains[1],
    )


def solution(mesh):
    return jax.shard_map(
        on_device,
        mesh=mesh,
        in_specs=(
            P(("dp", "mp"), None),
            P("dp", None),
            P(("dp", "mp"), None),
            P(),
            P(),
            P("dp", None, "mp"),
            P("mp", "dp"),
            P("dp", None, "mp"),
            P("mp", "dp"),
        ),
        out_specs=(
            P(("dp", "mp"), None),
            P(("dp", "mp"), None),
            P("dp", None, "mp"),
            P("mp", "dp"),
            P("dp", None, "mp"),
            P("mp", "dp"),
            P(),
            P(),
        ),
        check_vma=False,
    )
```
